32 devices in a mesh: ex: 8 (over z, y), ckpt: 4 (over x, core).
Axes of the slice: x: 2, y: 2, z: 4, core: 2. Of those that a mesh axis runs over, the one named last changes fastest.
Arguments:
- grads: bfloat16 [4, 2560, 4096], P('ckpt', 'ex'), may hold values from -6 to 6
- second_moment: float32 [4, 4096], P('ckpt'), may hold values from 0.25 to 4
- step_size: float32 [4], P('ckpt'), may hold values from 0.25 to 1
- partners: int32 [8, 2], P('ex'), may hold values from -1 to 7, as said below
- counts: int32 [8], P('ex'), may hold values from 1 to 2, as said below
Outputs:
- band_rows: float32 [2560, 1280], P('ex', 'ckpt')
The draws below stay inside these ranges and needn't reach their ends.
Inputs may be any that keep to these rules, and one draw needn't show every extreme that they name: For s < counts[b], partners[b, s] are distinct blocks among (b + 1) mod 8 to (b + 2) mod 8; slots from counts[b] on hold -1. `counts`: some block has 2 live slots in every draw.
All inputs are finite; a program needn't handle non-finite values.
Results may differ from the reference program's by a relative error of at most 0.0029.
Values may be sent and summed in bfloat16 or wider, within the bound.
A program may use at most 64 MiB of HBM per device.

```python
import math
import jax
import jax.numpy as jnp
from jax import lax

P_SIZE = 4096
BR = 320
CKPT = 4
BLOCKS = 8
EXAMPLES = 2560
REACH = 2


def pair_layout(key):
    base = jax.random.fold_in(key, 7)
    first_key, second_key, third_key = jax.random.split(base, 3)
    shifts = jax.random.randint(first_key, (BLOCKS,), 0, 4)
    amounts = jnp.maximum(jnp.right_shift(jnp.int32(REACH), shifts.astype(jnp.int32)), 1)
    busiest = jax.random.randint(second_key, (), 0, BLOCKS)
    amounts = jnp.where(jnp.arange(BLOCKS) == busiest, REACH, amounts).astype(jnp.int32)
    row_keys = jax.random.split(third_key, BLOCKS)
    orders = jax.vmap(lambda row_key: jax.random.permutation(row_key, REACH))(row_keys).astype(jnp.int32) + 1
    partner_ids = jnp.mod(jnp.arange(BLOCKS, dtype=jnp.int32)[:, None] + orders, BLOCKS)
    alive_slot = jnp.arange(REACH, dtype=jnp.int32)[None, :] < amounts[:, None]
    partner_ids = jnp.where(alive_slot, partner_ids, -1).astype(jnp.int32)
    return (partner_ids, amounts)


def draw_partners(key, part):
    return pair_layout(key)[0]


def draw_counts(key, part):
    return pair_layout(key)[1]


def steps_of(rng, extent, cuts, low, largest):
    level = 1.0
    for position, shards_of in cuts:
        heights = jax.random.uniform(jax.random.fold_in(jax.random.fold_in(rng, 6), position), (shards_of,), jnp.float32, low / len(cuts), largest / len(cuts))
        level = level * jnp.repeat(jnp.exp(heights), extent[position] // shards_of).reshape((-1,) + (1,) * (len(extent) - 1 - position))
    return level


def scatter_about(rng, dims, deviation, most, shards=(), kind=jnp.bfloat16):
    level = steps_of(rng, dims, shards, -0.22, 0.18) if shards else 1.0
    array = jax.random.normal(rng, dims, jnp.float32) * deviation * level
    return jnp.minimum(jnp.maximum(array, -most), most).astype(kind)


def setup_inputs(seed: int = 0) -> dict:
    streams_of = jax.random.split(jax.random.key(seed), 6)
    grads = scatter_about(streams_of[0], (CKPT, EXAMPLES, P_SIZE), 1.0, 6.0, ((0, 4), (1, 8)))
    second_moment = jnp.clip(jnp.exp(math.log(4.0) - 2.7725887 * jax.random.uniform(streams_of[1], (CKPT, P_SIZE), jnp.float32) ** steps_of(streams_of[1], (CKPT, P_SIZE), ((0, 4),), -0.2, 0.2)), 0.25, 4.0)
    step_size = jnp.clip(jnp.exp(math.log(1.0) - 1.3862944 * jax.random.uniform(streams_of[2], (CKPT,), jnp.float32) ** steps_of(streams_of[2], (CKPT,), ((0, 4),), -0.2, 0.2)), 0.25, 1.0)
    partners = draw_partners(jax.random.fold_in(streams_of[5], 71), 0)
    counts = draw_counts(jax.random.fold_in(streams_of[5], 71), 0)
    return dict(grads=grads, second_moment=second_moment, step_size=step_size, partners=partners, counts=counts)


EPSILON = 1e-08

def reference(grads, second_moment, step_size, partners, counts):
    factor = step_size[:, None] / (jnp.sqrt(second_moment) + EPSILON) * P_SIZE ** (-0.5)
    scaled = (grads.astype(jnp.float32) * factor[:, None, :]).astype(jnp.bfloat16)
    blocks = BLOCKS
    alive_slot = jnp.arange(REACH, dtype=jnp.int32)[None, :] < counts[:, None]
    offsets = jnp.mod(partners - jnp.arange(blocks, dtype=jnp.int32)[:, None], blocks)
    left_side = scaled.reshape(CKPT, blocks, BR, P_SIZE)
    right_side = grads.reshape(CKPT, blocks, BR, P_SIZE)
    forward = []
    backward = []
    for offset in range(1, REACH + 1):
        matched = jnp.logical_and(offsets == offset, alive_slot)
        listed = lax.optimization_barrier(jnp.sum(matched.astype(jnp.int32), axis=1))
        partner_rows = jnp.roll(right_side, -offset, axis=1)

        def add_checkpoint(running, operands):
            product = jnp.einsum('nrp,nsp->nrs', operands[0].astype(jnp.float32), operands[1].astype(jnp.float32))
            return (running + product, None)
        tile_set, unused = lax.scan(add_checkpoint, jnp.zeros((blocks, BR, BR), jnp.float32), (left_side, partner_rows))
        tile_set = tile_set * listed.astype(jnp.float32)[:, None, None]
        forward.append(tile_set)
        backward.insert(0, jnp.transpose(jnp.roll(tile_set, offset, axis=0), (0, 2, 1)))
    band_rows = jnp.stack(backward + forward, axis=2)
    return band_rows.reshape(blocks * BR, 2 * REACH * BR)
```

```python
import functools

import jax
import jax.numpy as jnp
from jax import lax
from jax.experimental import pallas as pl
from jax.experimental.pallas import tpu as pltpu
from jax.sharding import PartitionSpec as P

EPSILON = 1e-08
MESH = pl.DeviceIdType.MESH
PIECES = 8


def passed_along(value, axis, by):
    length = lax.axis_size(axis)
    return lax.ppermute(value, axis, [(i, (i + by) % length) for i in range(length)])


def general(grads, second_moment, step_size, partners, counts):
    width = grads.shape[2]
    block_rows = grads.shape[1]
    reach = partners.shape[1]
    blocks = lax.axis_size("ex")
    position = lax.axis_index("ex")
    factor = step_size[:, None] / (jnp.sqrt(second_moment) + EPSILON) * width ** (-0.5)
    scaled = (grads.astype(jnp.float32) * factor[:, None, :]).astype(jnp.bfloat16)
    offsets = jnp.mod(partners[0] - position, blocks)
    alive_slot = jnp.arange(reach, dtype=jnp.int32) < counts[0]
    wanted = jnp.arange(1, reach + 1, dtype=jnp.int32)
    matched = jnp.logical_and(offsets[:, None] == wanted[None, :], alive_slot[:, None])
    listed = jnp.sum(matched.astype(jnp.float32), axis=0)
    forward_list = []
    for offset in range(1, reach + 1):
        visitor = passed_along(grads, "ex", -offset)
        forward_list.append(
            lax.dot_general(
                scaled, visitor, (((0, 2), (0, 2)), ((), ())), preferred_element_type=jnp.float32
            )
            * listed[offset - 1]
        )
    stacked = jnp.stack(forward_list, axis=1)
    returned = []
    for offset in range(reach, 0, -1):
        arrived = passed_along(stacked[:, offset - 1, :], "ex", offset)
        returned.append(arrived.T)
    panel = jnp.concatenate([jnp.stack(returned, axis=1), stacked], axis=1)
    panel = panel.reshape(block_rows, 2 * reach * block_rows)
    return lax.psum_scatter(panel, "ckpt", scatter_dimension=1, tiled=True)


def kernel(
    blocks, reach, g_ref, moment_ref, step_ref, partners_ref, counts_ref, out_ref,
    own, oth, early, late, factor, acc, half, quarter, piece, half_in, quarter_in, parts,
    flag_own, flag_in, turned,
    own_sem, y_send, y_recv, e_send, e_recv, l_send, l_recv,
    h_send, h_recv, q_send, q_recv, p_send, parts_recv, f_send, f_recv,
):
    rows, width = g_ref.shape
    layers = blocks // 2
    span = width // 2
    piece_width = span // PIECES
    half_rows, quarter_rows = rows // 2, rows // 4
    e = lax.axis_index("ex")
    c = lax.axis_index("ckpt")
    z, y = e // 2, e % 2
    core, x = c % 2, c // 2

    mate = (2 * z + 1 - y, c)
    ahead = ((e + 2 * (2 * y - 1) + blocks) % blocks, c)
    behind = ((e - 2 * (2 * y - 1) + blocks) % blocks, c)
    core_mate = (e, c + 1 - 2 * core)
    x_mate = (e, (c + 2) % 4)
    offset = 2 - ((c + 1) // 2) % 2
    flag_to = ((e + offset) % blocks, c)
    flag_from = ((e - offset + blocks) % blocks, c)

    def owners(slot):
        a, o = [(2 * z, 1), (2 * z - y, 2), (2 * z + 1 - 2 * y, 1), (2 * z - 1 + y, 2)][slot]
        a = (a + blocks) % blocks
        return (a, reach - 1 + o), ((a + o) % blocks, reach - o)

    tile_row = (e - (1 - x) * offset + blocks) % blocks
    odd = tile_row % 2
    sources = []
    for row in range(2):
        layer = (tile_row // 2 + odd * ((offset - 1) + (2 - offset) * row)) % layers
        sources += [(2 * layer + row, q) for q in range(4)]

    barrier = pltpu.get_barrier_semaphore()

    for device in [mate, ahead, behind, core_mate, x_mate, flag_from] + sources:
        pl.semaphore_signal(barrier, inc=1, device_id=device, device_id_type=MESH)

    mine = pl.multiple_of(y * span, 128)
    theirs = pl.multiple_of((1 - y) * span, 128)
    own_copies = [
        pltpu.make_async_copy(
            g_ref.at[:, pl.ds(mine + j * piece_width, piece_width)], own.at[j], own_sem.at[j]
        )
        for j in range(PIECES)
    ]
    for copy in own_copies:
        copy.start()

    total = jnp.float32(0)
    for s in range(reach):
        apart = (partners_ref[0, s] - e + blocks) % blocks
        live = jnp.logical_and(apart == offset, s < counts_ref[0])
        total = total + jnp.where(live, jnp.float32(1), jnp.float32(0))
    flag_own[...] = jnp.full(flag_own.shape, total, jnp.float32)
    scale = step_ref[0] / (jnp.sqrt(moment_ref[:, pl.ds(mine, span)]) + EPSILON) * width ** (-0.5)
    for j in range(PIECES):
        factor[j] = scale[:, j * piece_width : (j + 1) * piece_width]

    pl.semaphore_wait(barrier, 14)

    def remote(src, dst, send, recv, device):
        return pltpu.make_async_remote_copy(
            src_ref=src, dst_ref=dst, send_sem=send, recv_sem=recv, device_id=device, device_id_type=MESH
        )

    flag_copy = remote(flag_own, flag_in, f_send, f_recv, flag_to)
    y_copies, e_copies, l_copies = [], [], []
    for j in range(PIECES):
        y_copies.append(
            remote(
                g_ref.at[:, pl.ds(theirs + j * piece_width, piece_width)],
                oth.at[j], y_send.at[j], y_recv.at[j], mate,
            )
        )
        e_copies.append(
            remote(
                g_ref.at[:, pl.ds(mine + j * piece_width, piece_width)],
                early.at[j], e_send.at[j], e_recv.at[j], ahead,
            )
        )
        l_copies.append(remote(oth.at[j], late.at[j], l_send.at[j], l_recv.at[j], behind))
    for j in range(PIECES):
        y_copies[j].start()
        e_copies[j].start()
    flag_copy.start()

    def add(slot, j, left, right, first):
        lhs = (left[j].astype(jnp.float32) * factor[j]).astype(jnp.bfloat16)
        product = lax.dot_general(
            lhs, right[j], (((1,), (1,)), ((), ())), preferred_element_type=jnp.float32
        )
        if first:
            acc[slot] = product
        else:
            acc[slot] += product

    def tiles(todo, j, first):
        @pl.when(y == 0)
        def _():
            for slot, left, right in todo:
                add(slot, j, left, right, first)

        @pl.when(y == 1)
        def _():
            for slot, left, right in todo:
                add(slot, j, right, left, first)

    def over_pieces(todo, arrive):
        arrive(0)
        tiles(todo, 0, True)

        def body(j, carry):
            arrive(j)
            tiles(todo, j, False)
            return carry

        lax.fori_loop(1, PIECES, body, 0)

    for copy in own_copies:
        copy.wait()

    def y_arrive(j):
        remote(oth.at[j], oth.at[j], y_send.at[j], y_recv.at[j], mate).wait_recv()

    over_pieces([(0, own, oth)], y_arrive)
    for copy in l_copies:
        copy.start()

    def e_arrive(j):
        remote(early.at[j], early.at[j], e_send.at[j], e_recv.at[j], ahead).wait_recv()

    over_pieces([(1, own, early), (2, oth, early)], e_arrive)

    def reduce_and_deliver(slots):
        low, high = slots[0], len(slots)
        group = pl.ds(low, high)
        keep = pl.multiple_of(core * half_rows, 16)
        give = pl.multiple_of((1 - core) * half_rows, 16)
        for t in slots:
            half[t] = acc[t, pl.ds(give, half_rows), :]
        first = remote(half.at[group], half_in.at[group], h_send.at[low], h_recv.at[low], core_mate)
        first.start()
        first.wait_recv()
        keep_x = pl.multiple_of(x * quarter_rows, 16)
        give_x = pl.multiple_of((1 - x) * quarter_rows, 16)
        for t in slots:
            quarter[t] = acc[t, pl.ds(keep + give_x, quarter_rows), :] + half_in[t, pl.ds(give_x, quarter_rows), :]
        second = remote(
            quarter.at[group], quarter_in.at[group], q_send.at[low], q_recv.at[low], x_mate
        )
        second.start()
        for t in slots:
            piece[t] = acc[t, pl.ds(keep + keep_x, quarter_rows), :] + half_in[t, pl.ds(keep_x, quarter_rows), :]
        second.wait_recv()
        for t in slots:
            piece[t] += quarter_in[t]
        for t in slots:
            for i, device in enumerate(owners(t)):
                here = jnp.logical_and(device[0] == e, device[1] == c)
                spot = parts.at[y, c]

                @pl.when(here)
                def _():
                    pltpu.make_async_copy(piece.at[t], spot, parts_recv.at[y, c]).start()

                @pl.when(jnp.logical_not(here))
                def _():
                    remote(piece.at[t], spot, p_send.at[t, i], parts_recv.at[y, c], device).start()

        def finish():
            first.wait_send()
            second.wait_send()
            for t in slots:
                for i, device in enumerate(owners(t)):
                    here = jnp.logical_and(device[0] == e, device[1] == c)

                    @pl.when(jnp.logical_not(here))
                    def _():
                        remote(
                            piece.at[t], parts.at[y, c], p_send.at[t, i], parts_recv.at[y, c], device
                        ).wait_send()

        return finish

    finish_early = reduce_and_deliver((0, 1, 2))

    def l_arrive(j):
        remote(late.at[j], late.at[j], l_send.at[j], l_recv.at[j], behind).wait_recv()

    over_pieces([(3, late, oth)], l_arrive)
    finish_late = reduce_and_deliver((3,))

    flag_copy.wait_recv()
    for row in range(2):
        for q in range(4):
            spot = parts.at[row, q]
            remote(spot, spot, p_send.at[0, 0], parts_recv.at[row, q], mate).wait_recv()
    for q in range(4):
        start = (q % 2) * half_rows + (q // 2) * quarter_rows
        turned[start : start + quarter_rows, :] = parts[0, q] + parts[1, q]

    @pl.when(c < reach)
    def _():
        out_ref[...] = turned[...].T * flag_in[0:1, 0:1]

    @pl.when(c >= reach)
    def _():
        out_ref[...] = turned[...] * flag_own[0:1, 0:1]

    for j in range(PIECES):
        y_copies[j].wait_send()
        e_copies[j].wait_send()
        l_copies[j].wait_send()
    flag_copy.wait_send()
    finish_early()
    finish_late()


def fused(grads, second_moment, step_size, partners, counts):
    rows, width = grads.shape[1:]
    reach = partners.shape[1]
    blocks = lax.axis_size("ex")
    piece_width = width // 2 // PIECES
    dma = pltpu.SemaphoreType.DMA
    vmem = pl.BlockSpec(memory_space=pltpu.VMEM)
    smem = pl.BlockSpec(memory_space=pltpu.SMEM)
    gradients = pltpu.VMEM((PIECES, rows, piece_width), jnp.bfloat16)
    return pl.pallas_call(
        functools.partial(kernel, blocks, reach),
        out_shape=jax.ShapeDtypeStruct((rows, rows), jnp.float32),
        in_specs=[pl.BlockSpec(memory_space=pl.ANY), vmem, smem, smem, smem],
        out_specs=vmem,
        scratch_shapes=[
            gradients, gradients, gradients, gradients,
            pltpu.VMEM((PIECES, 1, piece_width), jnp.float32),
            pltpu.VMEM((4, rows, rows), jnp.float32),
            pltpu.VMEM((4, rows // 2, rows), jnp.float32),
            pltpu.VMEM((4, rows // 4, rows), jnp.float32),
            pltpu.VMEM((4, rows // 4, rows), jnp.float32),
            pltpu.VMEM((4, rows // 2, rows), jnp.float32),
            pltpu.VMEM((4, rows // 4, rows), jnp.float32),
            pltpu.VMEM((2, 4, rows // 4, rows), jnp.float32),
            pltpu.VMEM((8, 128), jnp.float32),
            pltpu.VMEM((8, 128), jnp.float32),
            pltpu.VMEM((rows, rows), jnp.float32),
            dma((PIECES,)), dma((PIECES,)), dma((PIECES,)), dma((PIECES,)), dma((PIECES,)),
            dma((PIECES,)), dma((PIECES,)),
            dma((4,)), dma((4,)), dma((4,)), dma((4,)), dma((4, 2)), dma((2, 4)),
            dma, dma,
        ],
        compiler_params=pltpu.CompilerParams(collective_id=0, has_side_effects=True),
    )(grads[0], second_moment, step_size, partners, counts)


def local(grads, second_moment, step_size, partners, counts):
    rows, width = grads.shape[1:]
    blocks, ckpts = lax.axis_size("ex"), lax.axis_size("ckpt")
    fits = partners.shape[1] == 2 and ckpts == 4 and blocks % 2 == 0 and blocks >= 6
    fits = fits and rows % 64 == 0 and width % (256 * PIECES) == 0
    body = fused if fits else general
    return body(grads, second_moment, step_size, partners, counts)


def solution(mesh):
    in_specs = (P("ckpt", "ex", None), P("ckpt", None), P("ckpt"), P("ex", None), P("ex"))
    out_specs = P("ex", "ckpt")
    return jax.shard_map(local, mesh=mesh, in_specs=in_specs, out_specs=out_specs, check_vma=False)
```

```python
import functools

import jax
import jax.numpy as jnp
from jax import lax
from jax.experimental import pallas as pl
from jax.experimental.pallas import tpu as pltpu
from jax.sharding import PartitionSpec as P

EPSILON = 1e-08
MESH = pl.DeviceIdType.MESH
PIECES = 8


def passed_along(value, axis, by):
    length = lax.axis_size(axis)
    return lax.ppermute(value, axis, [(i, (i + by) % length) for i in range(length)])


def general(grads, second_moment, step_size, partners, counts):
    width = grads.shape[2]
    block_rows = grads.shape[1]
    reach = partners.shape[1]
    blocks = lax.axis_size("ex")
    position = lax.axis_index("ex")
    factor = step_size[:, None] / (jnp.sqrt(second_moment) + EPSILON) * width ** (-0.5)
    scaled = (grads.astype(jnp.float32) * factor[:, None, :]).astype(jnp.bfloat16)
    offsets = jnp.mod(partners[0] - position, blocks)
    alive_slot = jnp.arange(reach, dtype=jnp.int32) < counts[0]
    wanted = jnp.arange(1, reach + 1, dtype=jnp.int32)
    matched = jnp.logical_and(offsets[:, None] == wanted[None, :], alive_slot[:, None])
    listed = jnp.sum(matched.astype(jnp.float32), axis=0)
    forward_list = []
    for offset in range(1, reach + 1):
        visitor = passed_along(grads, "ex", -offset)
        forward_list.append(
            lax.dot_general(
                scaled, visitor, (((0, 2), (0, 2)), ((), ())), preferred_element_type=jnp.float32
            )
            * listed[offset - 1]
        )
    stacked = jnp.stack(forward_list, axis=1)
    returned = []
    for offset in range(reach, 0, -1):
        arrived = passed_along(stacked[:, offset - 1, :], "ex", offset)
        returned.append(arrived.T)
    panel = jnp.concatenate([jnp.stack(returned, axis=1), stacked], axis=1)
    panel = panel.reshape(block_rows, 2 * reach * block_rows)
    return lax.psum_scatter(panel, "ckpt", scatter_dimension=1, tiled=True)


def kernel(
    blocks, reach, g_ref, moment_ref, step_ref, partners_ref, counts_ref, out_ref,
    own, oth, early, late, factor, acc, half, quarter, piece, half_in, quarter_in, parts,
    flag_own, flag_in, turned,
    own_sem, y_send, y_recv, e_send, e_recv, l_send, l_recv,
    h_send, h_recv, q_send, q_recv, p_send, parts_recv, f_send, f_recv,
):
    rows, width = g_ref.shape
    layers = blocks // 2
    span = width // 2
    piece_width = span // PIECES
    half_rows, quarter_rows = rows // 2, rows // 4
    e = lax.axis_index("ex")
    c = lax.axis_index("ckpt")
    z, y = e // 2, e % 2
    core, x = c % 2, c // 2

    mate = (2 * z + 1 - y, c)
    ahead = ((e + 2 * (2 * y - 1) + blocks) % blocks, c)
    behind = ((e - 2 * (2 * y - 1) + blocks) % blocks, c)
    core_mate = (e, c + 1 - 2 * core)
    x_mate = (e, (c + 2) % 4)
    offset = 2 - ((c + 1) // 2) % 2
    flag_to = ((e + offset) % blocks, c)
    flag_from = ((e - offset + blocks) % blocks, c)

    def owners(slot):
        a, o = [(2 * z, 1), (2 * z - y, 2), (2 * z + 1 - 2 * y, 1), (2 * z - 1 + y, 2)][slot]
        a = (a + blocks) % blocks
        return (a, reach - 1 + o), ((a + o) % blocks, reach - o)

    tile_row = (e - (1 - x) * offset + blocks) % blocks
    odd = tile_row % 2
    sources = []
    for row in range(2):
        layer = (tile_row // 2 + odd * ((offset - 1) + (2 - offset) * row)) % layers
        sources += [(2 * layer + row, q) for q in range(4)]

    barrier = pltpu.get_barrier_semaphore()

    for device in [mate, ahead, behind, core_mate, x_mate, flag_from] + sources:
        pl.semaphore_signal(barrier, inc=1, device_id=device, device_id_type=MESH)

    mine = pl.multiple_of(y * span, 128)
    theirs = pl.multiple_of((1 - y) * span, 128)
    own_copies = [
        pltpu.make_async_copy(
            g_ref.at[:, pl.ds(mine + j * piece_width, piece_width)], own.at[j], own_sem.at[j]
        )
        for j in range(PIECES)
    ]
    for copy in own_copies:
        copy.start()

    total = jnp.float32(0)
    for s in range(reach):
        apart = (partners_ref[0, s] - e + blocks) % blocks
        live = jnp.logical_and(apart == offset, s < counts_ref[0])
        total = total + jnp.where(live, jnp.float32(1), jnp.float32(0))
    flag_own[...] = jnp.full(flag_own.shape, total, jnp.float32)
    scale = step_ref[0] / (jnp.sqrt(moment_ref[:, pl.ds(mine, span)]) + EPSILON) * width ** (-0.5)
    for j in range(PIECES):
        factor[j] = scale[:, j * piece_width : (j + 1) * piece_width]

    pl.semaphore_wait(barrier, 14)

    def remote(src, dst, send, recv, device):
        return pltpu.make_async_remote_copy(
            src_ref=src, dst_ref=dst, send_sem=send, recv_sem=recv, device_id=device, device_id_type=MESH
        )

    flag_copy = remote(flag_own, flag_in, f_send, f_recv, flag_to)
    y_copies, e_copies, l_copies = [], [], []
    for j in range(PIECES):
        y_copies.append(
            remote(
                g_ref.at[:, pl.ds(theirs + j * piece_width, piece_width)],
                oth.at[j], y_send.at[j], y_recv.at[j], mate,
            )
        )
        e_copies.append(
            remote(
                g_ref.at[:, pl.ds(mine + j * piece_width, piece_width)],
                early.at[j], e_send.at[j], e_recv.at[j], ahead,
            )
        )
        l_copies.append(remote(oth.at[j], late.at[j], l_send.at[j], l_recv.at[j], behind))
    for j in range(PIECES):
        y_copies[j].start()
        e_copies[j].start()
    flag_copy.start()

    def add(slot, j, left, right, first):
        lhs = (left[j].astype(jnp.float32) * factor[j]).astype(jnp.bfloat16)
        product = lax.dot_general(
            lhs, right[j], (((1,), (1,)), ((), ())), preferred_element_type=jnp.float32
        )
        if first:
            acc[slot] = product
        else:
            acc[slot] += product

    def tiles(todo, j, first):
        @pl.when(y == 0)
        def _():
            for slot, left, right in todo:
                add(slot, j, left, right, first)

        @pl.when(y == 1)
        def _():
            for slot, left, right in todo:
                add(slot, j, right, left, first)

    def over_pieces(todo, arrive):
        arrive(0)
        tiles(todo, 0, True)

        def body(j, carry):
            arrive(j)
            tiles(todo, j, False)
            return carry

        lax.fori_loop(1, PIECES, body, 0)

    for copy in own_copies:
        copy.wait()

    def y_arrive(j):
        remote(oth.at[j], oth.at[j], y_send.at[j], y_recv.at[j], mate).wait_recv()

    over_pieces([(0, own, oth)], y_arrive)
    for copy in l_copies:
        copy.start()

    def e_arrive(j):
        remote(early.at[j], early.at[j], e_send.at[j], e_recv.at[j], ahead).wait_recv()

    over_pieces([(1, own, early), (2, oth, early)], e_arrive)

    def reduce_and_deliver(slots):
        low, high = slots[0], len(slots)
        group = pl.ds(low, high)
        keep = pl.multiple_of(core * half_rows, 16)
        give = pl.multiple_of((1 - core) * half_rows, 16)
        for t in slots:
            half[t] = acc[t, pl.ds(give, half_rows), :]
        first = remote(half.at[group], half_in.at[group], h_send.at[low], h_recv.at[low], core_mate)
        first.start()
        first.wait_recv()
        keep_x = pl.multiple_of(x * quarter_rows, 16)
        give_x = pl.multiple_of((1 - x) * quarter_rows, 16)
        for t in slots:
            quarter[t] = acc[t, pl.ds(keep + give_x, quarter_rows), :] + half_in[t, pl.ds(give_x, quarter_rows), :]
        second = remote(
            quarter.at[group], quarter_in.at[group], q_send.at[low], q_recv.at[low], x_mate
        )
        second.start()
        second.wait_recv()
        for t in slots:
            kept = acc[t, pl.ds(keep + keep_x, quarter_rows), :] + half_in[t, pl.ds(keep_x, quarter_rows), :]
            piece[t] = (kept + quarter_in[t]).astype(piece.dtype)
        for t in slots:
            for i, device in enumerate(owners(t)):
                here = jnp.logical_and(device[0] == e, device[1] == c)
                spot = parts.at[y, c]

                @pl.when(here)
                def _():
                    pltpu.make_async_copy(piece.at[t], spot, parts_recv.at[y, c]).start()

                @pl.when(jnp.logical_not(here))
                def _():
                    remote(piece.at[t], spot, p_send.at[t, i], parts_recv.at[y, c], device).start()

        def finish():
            first.wait_send()
            second.wait_send()
            for t in slots:
                for i, device in enumerate(owners(t)):
                    here = jnp.logical_and(device[0] == e, device[1] == c)

                    @pl.when(jnp.logical_not(here))
                    def _():
                        remote(
                            piece.at[t], parts.at[y, c], p_send.at[t, i], parts_recv.at[y, c], device
                        ).wait_send()

        return finish

    finish_early = reduce_and_deliver((0, 1, 2))

    def l_arrive(j):
        remote(late.at[j], late.at[j], l_send.at[j], l_recv.at[j], behind).wait_recv()

    over_pieces([(3, late, oth)], l_arrive)
    finish_late = reduce_and_deliver((3,))

    flag_copy.wait_recv()
    for row in range(2):
        for q in range(4):
            spot = parts.at[row, q]
            remote(spot, spot, p_send.at[0, 0], parts_recv.at[row, q], mate).wait_recv()
    for q in range(4):
        start = (q % 2) * half_rows + (q // 2) * quarter_rows
        turned[start : start + quarter_rows, :] = parts[0, q].astype(jnp.float32) + parts[1, q].astype(jnp.float32)

    @pl.when(c < reach)
    def _():
        out_ref[...] = turned[...].T * flag_in[0:1, 0:1]

    @pl.when(c >= reach)
    def _():
        out_ref[...] = turned[...] * flag_own[0:1, 0:1]

    for j in range(PIECES):
        y_copies[j].wait_send()
        e_copies[j].wait_send()
        l_copies[j].wait_send()
    flag_copy.wait_send()
    finish_early()
    finish_late()


def fused(grads, second_moment, step_size, partners, counts):
    rows, width = grads.shape[1:]
    reach = partners.shape[1]
    blocks = lax.axis_size("ex")
    piece_width = width // 2 // PIECES
    dma = pltpu.SemaphoreType.DMA
    vmem = pl.BlockSpec(memory_space=pltpu.VMEM)
    smem = pl.BlockSpec(memory_space=pltpu.SMEM)
    gradients = pltpu.VMEM((PIECES, rows, piece_width), jnp.bfloat16)
    return pl.pallas_call(
        functools.partial(kernel, blocks, reach),
        out_shape=jax.ShapeDtypeStruct((rows, rows), jnp.float32),
        in_specs=[pl.BlockSpec(memory_space=pl.ANY), vmem, smem, smem, smem],
        out_specs=vmem,
        scratch_shapes=[
            gradients, gradients, gradients, gradients,
            pltpu.VMEM((PIECES, 1, piece_width), jnp.float32),
            pltpu.VMEM((4, rows, rows), jnp.float32),
            pltpu.VMEM((4, rows // 2, rows), jnp.float32),
            pltpu.VMEM((4, rows // 4, rows), jnp.float32),
            pltpu.VMEM((4, rows // 4, rows), jnp.bfloat16),
            pltpu.VMEM((4, rows // 2, rows), jnp.float32),
            pltpu.VMEM((4, rows // 4, rows), jnp.float32),
            pltpu.VMEM((2, 4, rows // 4, rows), jnp.bfloat16),
            pltpu.VMEM((8, 128), jnp.float32),
            pltpu.VMEM((8, 128), jnp.float32),
            pltpu.VMEM((rows, rows), jnp.float32),
            dma((PIECES,)), dma((PIECES,)), dma((PIECES,)), dma((PIECES,)), dma((PIECES,)),
            dma((PIECES,)), dma((PIECES,)),
            dma((4,)), dma((4,)), dma((4,)), dma((4,)), dma((4, 2)), dma((2, 4)),
            dma, dma,
        ],
        compiler_params=pltpu.CompilerParams(collective_id=0, has_side_effects=True),
    )(grads[0], second_moment, step_size, partners, counts)


def local(grads, second_moment, step_size, partners, counts):
    rows, width = grads.shape[1:]
    blocks, ckpts = lax.axis_size("ex"), lax.axis_size("ckpt")
    fits = partners.shape[1] == 2 and ckpts == 4 and blocks % 2 == 0 and blocks >= 6
    fits = fits and rows % 64 == 0 and width % (256 * PIECES) == 0
    body = fused if fits else general
    return body(grads, second_moment, step_size, partners, counts)


def solution(mesh):
    in_specs = (P("ckpt", "ex", None), P("ckpt", None), P("ckpt"), P("ex", None), P("ex"))
    out_specs = P("ex", "ckpt")
    return jax.shard_map(local, mesh=mesh, in_specs=in_specs, out_specs=out_specs, check_vma=False)
```

```python
import functools

import jax
import jax.numpy as jnp
from jax import lax
from jax.experimental import pallas as pl
from jax.experimental.pallas import tpu as pltpu
from jax.sharding import PartitionSpec as P

EPSILON = 1e-08
MESH = pl.DeviceIdType.MESH
PIECES = 8
ROUND_ROWS = 64


def passed_along(value, axis, by):
    length = lax.axis_size(axis)
    return lax.ppermute(value, axis, [(i, (i + by) % length) for i in range(length)])


def general(grads, second_moment, step_size, partners, counts):
    width = grads.shape[2]
    block_rows = grads.shape[1]
    reach = partners.shape[1]
    blocks = lax.axis_size("ex")
    position = lax.axis_index("ex")
    factor = step_size[:, None] / (jnp.sqrt(second_moment) + EPSILON) * width ** (-0.5)
    scaled = (grads.astype(jnp.float32) * factor[:, None, :]).astype(jnp.bfloat16)
    offsets = jnp.mod(partners[0] - position, blocks)
    alive_slot = jnp.arange(reach, dtype=jnp.int32) < counts[0]
    wanted = jnp.arange(1, reach + 1, dtype=jnp.int32)
    matched = jnp.logical_and(offsets[:, None] == wanted[None, :], alive_slot[:, None])
    listed = jnp.sum(matched.astype(jnp.float32), axis=0)
    forward_list = []
    for offset in range(1, reach + 1):
        visitor = passed_along(grads, "ex", -offset)
        forward_list.append(
            lax.dot_general(
                scaled, visitor, (((0, 2), (0, 2)), ((), ())), preferred_element_type=jnp.float32
            )
            * listed[offset - 1]
        )
    stacked = jnp.stack(forward_list, axis=1)
    returned = []
    for offset in range(reach, 0, -1):
        arrived = passed_along(stacked[:, offset - 1, :], "ex", offset)
        returned.append(arrived.T)
    panel = jnp.concatenate([jnp.stack(returned, axis=1), stacked], axis=1)
    panel = panel.reshape(block_rows, 2 * reach * block_rows)
    return lax.psum_scatter(panel, "ckpt", scatter_dimension=1, tiled=True)


def kernel(
    blocks, reach, g_ref, moment_ref, step_ref, partners_ref, counts_ref, out_ref,
    own, oth, early, late, factor, acc, half, quarter, piece, half_in, quarter_in, parts,
    flag_own, flag_in, turned, ready, slab, slab_in, late_piece, late_parts, late_sum,
    own_sem, y_send, y_recv, e_send, e_recv, l_send, l_recv,
    h_send, h_recv, q_send, q_recv, p_send, parts_recv, f_send, f_recv,
    x_send, x_recv, lp_send, late_recv,
):
    rows, width = g_ref.shape
    layers = blocks // 2
    span = width // 2
    piece_width = span // PIECES
    half_rows, quarter_rows = rows // 2, rows // 4
    rounds, share = rows // ROUND_ROWS, ROUND_ROWS // 4
    e = lax.axis_index("ex")
    c = lax.axis_index("ckpt")
    z, y = e // 2, e % 2
    core, x = c % 2, c // 2

    mate = (2 * z + 1 - y, c)
    ahead = ((e + 2 * (2 * y - 1) + blocks) % blocks, c)
    behind = ((e - 2 * (2 * y - 1) + blocks) % blocks, c)
    core_mate = (e, c + 1 - 2 * core)
    x_mate = (e, (c + 2) % 4)
    cross_mate = (e, (c + 3 - 2 * core) % 4)
    offset = 2 - ((c + 1) // 2) % 2
    flag_to = ((e + offset) % blocks, c)
    flag_from = ((e - offset + blocks) % blocks, c)

    def owners(slot):
        a, o = [(2 * z, 1), (2 * z - y, 2), (2 * z + 1 - 2 * y, 1), (2 * z - 1 + y, 2)][slot]
        a = (a + blocks) % blocks
        return (a, reach - 1 + o), ((a + o) % blocks, reach - o)

    tile_row = (e - (1 - x) * offset + blocks) % blocks
    odd = tile_row % 2
    sources = []
    for row in range(2):
        layer = (tile_row // 2 + odd * ((offset - 1) + (2 - offset) * row)) % layers
        sources += [(2 * layer + row, q) for q in range(4)]

    barrier = pltpu.get_barrier_semaphore()

    for device in [mate, ahead, behind, core_mate, x_mate, cross_mate, flag_from] + sources:
        pl.semaphore_signal(barrier, inc=1, device_id=device, device_id_type=MESH)

    mine = pl.multiple_of(y * span, 128)
    theirs = pl.multiple_of((1 - y) * span, 128)
    own_copies = [
        pltpu.make_async_copy(
            g_ref.at[:, pl.ds(mine + j * piece_width, piece_width)], own.at[j], own_sem.at[j]
        )
        for j in range(PIECES)
    ]
    for copy in own_copies:
        copy.start()

    total = jnp.float32(0)
    for s in range(reach):
        apart = (partners_ref[0, s] - e + blocks) % blocks
        live = jnp.logical_and(apart == offset, s < counts_ref[0])
        total = total + jnp.where(live, jnp.float32(1), jnp.float32(0))
    flag_own[...] = jnp.full(flag_own.shape, total, jnp.float32)
    scale = step_ref[0] / (jnp.sqrt(moment_ref[:, pl.ds(mine, span)]) + EPSILON) * width ** (-0.5)
    for j in range(PIECES):
        factor[j] = scale[:, j * piece_width : (j + 1) * piece_width]

    pl.semaphore_wait(barrier, 15)

    def remote(src, dst, send, recv, device):
        return pltpu.make_async_remote_copy(
            src_ref=src, dst_ref=dst, send_sem=send, recv_sem=recv, device_id=device, device_id_type=MESH
        )

    flag_copy = remote(flag_own, flag_in, f_send, f_recv, flag_to)
    y_copies, e_copies, l_copies = [], [], []
    for j in range(PIECES):
        y_copies.append(
            remote(
                g_ref.at[:, pl.ds(theirs + j * piece_width, piece_width)],
                oth.at[j], y_send.at[j], y_recv.at[j], mate,
            )
        )
        e_copies.append(
            remote(
                g_ref.at[:, pl.ds(mine + j * piece_width, piece_width)],
                early.at[j], e_send.at[j], e_recv.at[j], ahead,
            )
        )
    for r in range(rounds):
        part = oth.at[:, pl.ds(r * ROUND_ROWS, ROUND_ROWS), :]
        l_copies.append(remote(part, late.at[r], l_send.at[r], l_recv.at[r], behind))
    for j in range(PIECES):
        y_copies[j].start()
        e_copies[j].start()
    flag_copy.start()

    def add(slot, j, left, right, first):
        lhs = (left[j].astype(jnp.float32) * factor[j]).astype(jnp.bfloat16)
        product = lax.dot_general(
            lhs, right[j], (((1,), (1,)), ((), ())), preferred_element_type=jnp.float32
        )
        if first:
            acc[slot] = product
        else:
            acc[slot] += product

    def tiles(todo, j, first):
        @pl.when(y == 0)
        def _():
            for slot, left, right in todo:
                add(slot, j, left, right, first)

        @pl.when(y == 1)
        def _():
            for slot, left, right in todo:
                add(slot, j, right, left, first)

    def over_pieces(todo, arrive):
        arrive(0)
        tiles(todo, 0, True)

        def body(j, carry):
            arrive(j)
            tiles(todo, j, False)
            return carry

        lax.fori_loop(1, PIECES, body, 0)

    for copy in own_copies:
        copy.wait()

    def y_arrive(j):
        remote(oth.at[j], oth.at[j], y_send.at[j], y_recv.at[j], mate).wait_recv()

    over_pieces([(0, own, oth)], y_arrive)
    for copy in l_copies:
        copy.start()

    def e_arrive(j):
        remote(early.at[j], early.at[j], e_send.at[j], e_recv.at[j], ahead).wait_recv()

    over_pieces([(1, own, early), (2, oth, early)], e_arrive)

    def reduce_and_deliver(slots):
        low, high = slots[0], len(slots)
        group = pl.ds(low, high)
        keep = pl.multiple_of(core * half_rows, 16)
        give = pl.multiple_of((1 - core) * half_rows, 16)
        for t in slots:
            half[t] = acc[t, pl.ds(give, half_rows), :]
        first = remote(half.at[group], half_in.at[group], h_send.at[low], h_recv.at[low], core_mate)
        first.start()
        first.wait_recv()
        keep_x = pl.multiple_of(x * quarter_rows, 16)
        give_x = pl.multiple_of((1 - x) * quarter_rows, 16)
        for t in slots:
            quarter[t] = acc[t, pl.ds(keep + give_x, quarter_rows), :] + half_in[t, pl.ds(give_x, quarter_rows), :]
        second = remote(
            quarter.at[group], quarter_in.at[group], q_send.at[low], q_recv.at[low], x_mate
        )
        second.start()
        second.wait_recv()
        for t in slots:
            kept = acc[t, pl.ds(keep + keep_x, quarter_rows), :] + half_in[t, pl.ds(keep_x, quarter_rows), :]
            piece[t] = (kept + quarter_in[t]).astype(piece.dtype)
        for t in slots:
            for i, device in enumerate(owners(t)):
                here = jnp.logical_and(device[0] == e, device[1] == c)
                spot = parts.at[y, c]

                @pl.when(here)
                def _():
                    pltpu.make_async_copy(piece.at[t], spot, parts_recv.at[y, c]).start()

                @pl.when(jnp.logical_not(here))
                def _():
                    remote(piece.at[t], spot, p_send.at[t, i], parts_recv.at[y, c], device).start()

        def finish():
            first.wait_send()
            second.wait_send()
            for t in slots:
                for i, device in enumerate(owners(t)):
                    here = jnp.logical_and(device[0] == e, device[1] == c)

                    @pl.when(jnp.logical_not(here))
                    def _():
                        remote(
                            piece.at[t], parts.at[y, c], p_send.at[t, i], parts_recv.at[y, c], device
                        ).wait_send()

        return finish

    finish_early = reduce_and_deliver((0, 1, 2))

    @pl.when(y == 1)
    def _():
        def scale_piece(j, carry):
            ready[j] = (oth[j].astype(jnp.float32) * factor[j]).astype(jnp.bfloat16)
            return carry

        lax.fori_loop(0, PIECES, scale_piece, 0)

    def shares(r):
        out = []
        for d in range(1, 4):
            peer = (c + d) % 4
            given = slab.at[r, pl.ds(pl.multiple_of(peer * share, share), share), :]
            out.append(
                remote(given, slab_in.at[r, d - 1], x_send.at[r, d - 1], x_recv.at[r, d - 1], (e, peer))
            )
        return out

    def multiply(r):
        def product(lhs, rhs):
            return lax.dot_general(
                lhs, rhs, (((1,), (1,)), ((), ())), preferred_element_type=jnp.float32
            )

        @pl.when(y == 0)
        def _():
            total = jnp.zeros((ROUND_ROWS, rows), jnp.float32)
            for j in range(PIECES):
                lhs = (late[r, j].astype(jnp.float32) * factor[j]).astype(jnp.bfloat16)
                total = total + product(lhs, oth[j])
            slab[r] = total

        @pl.when(y == 1)
        def _():
            total = jnp.zeros((ROUND_ROWS, rows), jnp.float32)
            for j in range(PIECES):
                total = total + product(late[r, j], ready[j])
            slab[r] = total

    late_owners = owners(3)

    def deliver(r):
        for copy in shares(r):
            copy.wait_recv()
        total = slab[r, pl.ds(pl.multiple_of(c * share, share), share), :]
        for d in range(3):
            total = total + slab_in[r, d]
        late_piece[r] = total.astype(late_piece.dtype)
        for i, device in enumerate(late_owners):
            here = jnp.logical_and(device[0] == e, device[1] == c)
            spot = late_parts.at[r, c]

            @pl.when(here)
            def _():
                pltpu.make_async_copy(late_piece.at[r], spot, late_recv.at[r, c]).start()

            @pl.when(jnp.logical_not(here))
            def _():
                remote(late_piece.at[r], spot, lp_send.at[r, i], late_recv.at[r, c], device).start()

    def one_round(r, carry):
        remote(late.at[r], late.at[r], l_send.at[r], l_recv.at[r], behind).wait_recv()
        multiply(r)
        for copy in shares(r):
            copy.start()

        @pl.when(r > 0)
        def _():
            deliver(r - 1)

        return carry

    lax.fori_loop(0, rounds, one_round, 0)
    deliver(rounds - 1)

    flag_copy.wait_recv()

    def part_wait(row, q):
        spot = parts.at[row, q]
        remote(spot, spot, p_send.at[0, 0], parts_recv.at[row, q], mate).wait_recv()

    def quarter_at(q):
        start = (q % 2) * half_rows + (q // 2) * quarter_rows
        return slice(start, start + quarter_rows)

    @pl.when(offset == 1)
    def _():
        for q in range(4):
            part_wait(0, q)
            part_wait(1, q)
            both = parts[0, q].astype(jnp.float32) + parts[1, q].astype(jnp.float32)
            turned[quarter_at(q), :] = both

    @pl.when(offset == 2)
    def _():
        for q in range(4):
            part_wait(odd, q)
            turned[quarter_at(q), :] = parts[odd, q].astype(jnp.float32)
        for r in range(rounds):
            for q in range(4):
                spot = late_parts.at[r, q]
                remote(spot, spot, lp_send.at[0, 0], late_recv.at[r, q], mate).wait_recv()
                start = r * ROUND_ROWS + q * share
                late_sum[start : start + share, :] = late_parts[r, q].astype(jnp.float32)

    @pl.when(jnp.logical_and(offset == 2, odd == 1))
    def _():
        turned[...] += late_sum[...]

    flipped = jnp.logical_and(offset == 2, odd == 0)

    @pl.when(c < reach)
    def _():
        out_ref[...] = turned[...].T * flag_in[0:1, 0:1]

        @pl.when(flipped)
        def _():
            out_ref[...] += late_sum[...] * flag_in[0:1, 0:1]

    @pl.when(c >= reach)
    def _():
        out_ref[...] = turned[...] * flag_own[0:1, 0:1]

        @pl.when(flipped)
        def _():
            out_ref[...] += late_sum[...].T * flag_own[0:1, 0:1]

    for j in range(PIECES):
        y_copies[j].wait_send()
        e_copies[j].wait_send()
    flag_copy.wait_send()
    finish_early()
    for r in range(rounds):
        l_copies[r].wait_send()
        for copy in shares(r):
            copy.wait_send()
        for i, device in enumerate(late_owners):
            here = jnp.logical_and(device[0] == e, device[1] == c)

            @pl.when(jnp.logical_not(here))
            def _():
                remote(
                    late_piece.at[r], late_parts.at[r, c], lp_send.at[r, i], late_recv.at[r, c], device
                ).wait_send()


def fused(grads, second_moment, step_size, partners, counts):
    rows, width = grads.shape[1:]
    reach = partners.shape[1]
    blocks = lax.axis_size("ex")
    piece_width = width // 2 // PIECES
    dma = pltpu.SemaphoreType.DMA
    vmem = pl.BlockSpec(memory_space=pltpu.VMEM)
    smem = pl.BlockSpec(memory_space=pltpu.SMEM)
    rounds, share = rows // ROUND_ROWS, ROUND_ROWS // 4
    gradients = pltpu.VMEM((PIECES, rows, piece_width), jnp.bfloat16)
    return pl.pallas_call(
        functools.partial(kernel, blocks, reach),
        out_shape=jax.ShapeDtypeStruct((rows, rows), jnp.float32),
        in_specs=[pl.BlockSpec(memory_space=pl.ANY), vmem, smem, smem, smem],
        out_specs=vmem,
        scratch_shapes=[
            gradients, gradients, gradients,
            pltpu.VMEM((rounds, PIECES, ROUND_ROWS, piece_width), jnp.bfloat16),
            pltpu.VMEM((PIECES, 1, piece_width), jnp.float32),
            pltpu.VMEM((3, rows, rows), jnp.float32),
            pltpu.VMEM((4, rows // 2, rows), jnp.float32),
            pltpu.VMEM((4, rows // 4, rows), jnp.float32),
            pltpu.VMEM((4, rows // 4, rows), jnp.bfloat16),
            pltpu.VMEM((4, rows // 2, rows), jnp.float32),
            pltpu.VMEM((4, rows // 4, rows), jnp.float32),
            pltpu.VMEM((2, 4, rows // 4, rows), jnp.bfloat16),
            pltpu.VMEM((8, 128), jnp.float32),
            pltpu.VMEM((8, 128), jnp.float32),
            pltpu.VMEM((rows, rows), jnp.float32),
            gradients,
            pltpu.VMEM((rounds, ROUND_ROWS, rows), jnp.float32),
            pltpu.VMEM((rounds, 3, share, rows), jnp.float32),
            pltpu.VMEM((rounds, share, rows), jnp.bfloat16),
            pltpu.VMEM((rounds, 4, share, rows), jnp.bfloat16),
            pltpu.VMEM((rows, rows), jnp.float32),
            dma((PIECES,)), dma((PIECES,)), dma((PIECES,)), dma((PIECES,)), dma((PIECES,)),
            dma((rounds,)), dma((rounds,)),
            dma((4,)), dma((4,)), dma((4,)), dma((4,)), dma((4, 2)), dma((2, 4)),
            dma, dma,
            dma((rounds, 3)), dma((rounds, 3)), dma((rounds, 2)), dma((rounds, 4)),
        ],
        compiler_params=pltpu.CompilerParams(collective_id=0, has_side_effects=True),
    )(grads[0], second_moment, step_size, partners, counts)


def local(grads, second_moment, step_size, partners, counts):
    rows, width = grads.shape[1:]
    blocks, ckpts = lax.axis_size("ex"), lax.axis_size("ckpt")
    fits = partners.shape[1] == 2 and ckpts == 4 and blocks % 2 == 0 and blocks >= 6
    fits = fits and rows % 64 == 0 and width % (256 * PIECES) == 0
    body = fused if fits else general
    return body(grads, second_moment, step_size, partners, counts)


def solution(mesh):
    in_specs = (P("ckpt", "ex", None), P("ckpt", None), P("ckpt"), P("ex", None), P("ex"))
    out_specs = P("ex", "ckpt")
    return jax.shard_map(local, mesh=mesh, in_specs=in_specs, out_specs=out_specs, check_vma=False)
```

```python
import functools

import jax
import jax.numpy as jnp
from jax import lax
from jax.experimental import pallas as pl
from jax.experimental.pallas import tpu as pltpu
from jax.sharding import PartitionSpec as P

EPSILON = 1e-08
MESH = pl.DeviceIdType.MESH
PIECES = 8
ROUND_ROWS = 64


def passed_along(value, axis, by):
    length = lax.axis_size(axis)
    return lax.ppermute(value, axis, [(i, (i + by) % length) for i in range(length)])


def general(grads, second_moment, step_size, partners, counts):
    width = grads.shape[2]
    block_rows = grads.shape[1]
    reach = partners.shape[1]
    blocks = lax.axis_size("ex")
    position = lax.axis_index("ex")
    factor = step_size[:, None] / (jnp.sqrt(second_moment) + EPSILON) * width ** (-0.5)
    scaled = (grads.astype(jnp.float32) * factor[:, None, :]).astype(jnp.bfloat16)
    offsets = jnp.mod(partners[0] - position, blocks)
    alive_slot = jnp.arange(reach, dtype=jnp.int32) < counts[0]
    wanted = jnp.arange(1, reach + 1, dtype=jnp.int32)
    matched = jnp.logical_and(offsets[:, None] == wanted[None, :], alive_slot[:, None])
    listed = jnp.sum(matched.astype(jnp.float32), axis=0)
    forward_list = []
    for offset in range(1, reach + 1):
        visitor = passed_along(grads, "ex", -offset)
        forward_list.append(
            lax.dot_general(
                scaled, visitor, (((0, 2), (0, 2)), ((), ())), preferred_element_type=jnp.float32
            )
            * listed[offset - 1]
        )
    stacked = jnp.stack(forward_list, axis=1)
    returned = []
    for offset in range(reach, 0, -1):
        arrived = passed_along(stacked[:, offset - 1, :], "ex", offset)
        returned.append(arrived.T)
    panel = jnp.concatenate([jnp.stack(returned, axis=1), stacked], axis=1)
    panel = panel.reshape(block_rows, 2 * reach * block_rows)
    return lax.psum_scatter(panel, "ckpt", scatter_dimension=1, tiled=True)


def kernel(
    blocks, reach, g_ref, moment_ref, step_ref, partners_ref, counts_ref, out_ref,
    own, oth, early, late, factor, acc, half, quarter, piece, half_in, quarter_in, parts,
    flag_own, flag_in, turned, ready, slab, slab_in, late_piece, late_parts, extra,
    own_sem, y_send, y_recv, e_send, e_recv, l_send, l_recv,
    h_send, h_recv, q_send, q_recv, p_send, parts_recv, f_send, f_recv,
    x_send, x_recv, lp_send, late_recv, t_send, t_recv,
):
    rows, width = g_ref.shape
    layers = blocks // 2
    span = width // 2
    piece_width = span // PIECES
    half_rows, quarter_rows = rows // 2, rows // 4
    rounds, share = rows // ROUND_ROWS, ROUND_ROWS // 4
    e = lax.axis_index("ex")
    c = lax.axis_index("ckpt")
    z, y = e // 2, e % 2
    core, x = c % 2, c // 2

    mate = (2 * z + 1 - y, c)
    ahead = ((e + 2 * (2 * y - 1) + blocks) % blocks, c)
    behind = ((e - 2 * (2 * y - 1) + blocks) % blocks, c)
    core_mate = (e, c + 1 - 2 * core)
    x_mate = (e, (c + 2) % 4)
    cross_mate = (e, (c + 3 - 2 * core) % 4)
    offset = 2 - ((c + 1) // 2) % 2
    flag_to = ((e + offset) % blocks, c)
    flag_from = ((e - offset + blocks) % blocks, c)

    def owners(slot):
        a, o = [(2 * z, 1), (2 * z + 1 - 2 * y, 1), (2 * z - y, 2), (2 * z - 1 + y, 2)][slot]
        a = (a + blocks) % blocks
        return (a, reach - 1 + o), ((a + o) % blocks, reach - o)

    tile_row = (e - (1 - x) * offset + blocks) % blocks
    odd = tile_row % 2
    sources = []
    for row in range(2):
        layer = (tile_row // 2 + odd * ((offset - 1) + (2 - offset) * row)) % layers
        sources += [(2 * layer + row, q) for q in range(4)]

    barrier = pltpu.get_barrier_semaphore()

    for device in [mate, ahead, behind, core_mate, x_mate, cross_mate, flag_from] + sources:
        pl.semaphore_signal(barrier, inc=1, device_id=device, device_id_type=MESH)

    mine = pl.multiple_of(y * span, 128)
    theirs = pl.multiple_of((1 - y) * span, 128)
    own_copies = [
        pltpu.make_async_copy(
            g_ref.at[:, pl.ds(mine + j * piece_width, piece_width)], own.at[j], own_sem.at[j]
        )
        for j in range(PIECES)
    ]
    for copy in own_copies:
        copy.start()

    total = jnp.float32(0)
    for s in range(reach):
        apart = (partners_ref[0, s] - e + blocks) % blocks
        live = jnp.logical_and(apart == offset, s < counts_ref[0])
        total = total + jnp.where(live, jnp.float32(1), jnp.float32(0))
    flag_own[...] = jnp.full(flag_own.shape, total, jnp.float32)
    scale = step_ref[0] / (jnp.sqrt(moment_ref[:, pl.ds(mine, span)]) + EPSILON) * width ** (-0.5)
    for j in range(PIECES):
        factor[j] = scale[:, j * piece_width : (j + 1) * piece_width]

    pl.semaphore_wait(barrier, 15)

    def remote(src, dst, send, recv, device):
        return pltpu.make_async_remote_copy(
            src_ref=src, dst_ref=dst, send_sem=send, recv_sem=recv, device_id=device, device_id_type=MESH
        )

    flag_copy = remote(flag_own, flag_in, f_send, f_recv, flag_to)
    y_copies, e_copies, l_copies = [], [], []
    for j in range(PIECES):
        y_copies.append(
            remote(
                g_ref.at[:, pl.ds(theirs + j * piece_width, piece_width)],
                oth.at[j], y_send.at[j], y_recv.at[j], mate,
            )
        )
        e_copies.append(
            remote(
                g_ref.at[:, pl.ds(mine + j * piece_width, piece_width)],
                early.at[j], e_send.at[j], e_recv.at[j], ahead,
            )
        )
    for r in range(rounds):
        part = oth.at[:, pl.ds(r * ROUND_ROWS, ROUND_ROWS), :]
        l_copies.append(remote(part, late.at[r], l_send.at[r], l_recv.at[r], behind))
    for j in range(PIECES):
        y_copies[j].start()
        e_copies[j].start()
    flag_copy.start()

    def scaled(ref, j):
        return (ref[j].astype(jnp.float32) * factor[j]).astype(jnp.bfloat16)

    def add(slot, lhs, rhs, first):
        product = lax.dot_general(
            lhs, rhs, (((1,), (1,)), ((), ())), preferred_element_type=jnp.float32
        )
        if first:
            acc[slot] = product
        else:
            acc[slot] += product

    def tiles(todo, j, first):
        @pl.when(y == 0)
        def _():
            for slot, left, right in todo:
                if slot == 2:
                    add(slot, right[j], scaled(left, j), first)
                else:
                    add(slot, scaled(left, j), right[j], first)

        @pl.when(y == 1)
        def _():
            for slot, left, right in todo:
                add(slot, scaled(right, j), left[j], first)

    def over_pieces(todo, arrive):
        arrive(0)
        tiles(todo, 0, True)

        def body(j, carry):
            arrive(j)
            tiles(todo, j, False)
            return carry

        lax.fori_loop(1, PIECES, body, 0)

    for copy in own_copies:
        copy.wait()

    def y_arrive(j):
        remote(oth.at[j], oth.at[j], y_send.at[j], y_recv.at[j], mate).wait_recv()

    over_pieces([(0, own, oth)], y_arrive)
    for copy in l_copies:
        copy.start()

    def e_arrive(j):
        remote(early.at[j], early.at[j], e_send.at[j], e_recv.at[j], ahead).wait_recv()

    over_pieces([(2, own, early), (1, oth, early)], e_arrive)
    extra_copies = []
    for r in range(rounds):
        part = pl.ds(r * ROUND_ROWS, ROUND_ROWS)
        extra_copies.append(remote(acc.at[2, part, :], extra.at[r], t_send.at[r], t_recv.at[r], mate))
    for copy in extra_copies:
        copy.start()

    def reduce_and_deliver(slots):
        low, high = slots[0], len(slots)
        group = pl.ds(low, high)
        keep = pl.multiple_of(core * half_rows, 16)
        give = pl.multiple_of((1 - core) * half_rows, 16)
        for t in slots:
            half[t] = acc[t, pl.ds(give, half_rows), :]
        first = remote(half.at[group], half_in.at[group], h_send, h_recv, core_mate)
        first.start()
        first.wait_recv()
        keep_x = pl.multiple_of(x * quarter_rows, 16)
        give_x = pl.multiple_of((1 - x) * quarter_rows, 16)
        for t in slots:
            quarter[t] = acc[t, pl.ds(keep + give_x, quarter_rows), :] + half_in[t, pl.ds(give_x, quarter_rows), :]
        second = remote(
            quarter.at[group], quarter_in.at[group], q_send, q_recv, x_mate
        )
        second.start()
        second.wait_recv()
        for t in slots:
            kept = acc[t, pl.ds(keep + keep_x, quarter_rows), :] + half_in[t, pl.ds(keep_x, quarter_rows), :]
            piece[t] = (kept + quarter_in[t]).astype(piece.dtype)
        for t in slots:
            for i, device in enumerate(owners(t)):
                here = jnp.logical_and(device[0] == e, device[1] == c)
                spot = parts.at[y, c]

                @pl.when(here)
                def _():
                    pltpu.make_async_copy(piece.at[t], spot, parts_recv.at[y, c]).start()

                @pl.when(jnp.logical_not(here))
                def _():
                    remote(piece.at[t], spot, p_send.at[t, i], parts_recv.at[y, c], device).start()

        def finish():
            first.wait_send()
            second.wait_send()
            for t in slots:
                for i, device in enumerate(owners(t)):
                    here = jnp.logical_and(device[0] == e, device[1] == c)

                    @pl.when(jnp.logical_not(here))
                    def _():
                        remote(
                            piece.at[t], parts.at[y, c], p_send.at[t, i], parts_recv.at[y, c], device
                        ).wait_send()

        return finish

    finish_early = reduce_and_deliver((0, 1))

    @pl.when(y == 1)
    def _():
        def scale_piece(j, carry):
            ready[j] = (oth[j].astype(jnp.float32) * factor[j]).astype(jnp.bfloat16)
            return carry

        lax.fori_loop(0, PIECES, scale_piece, 0)

    def shares(r):
        out = []
        for d in range(1, 4):
            peer = (c + d) % 4
            given = slab.at[r, pl.ds(pl.multiple_of(peer * share, share), share), :]
            out.append(
                remote(given, slab_in.at[r, d - 1], x_send.at[r, d - 1], x_recv.at[r, d - 1], (e, peer))
            )
        return out

    def multiply(r):
        def product(lhs, rhs):
            return lax.dot_general(
                lhs, rhs, (((1,), (1,)), ((), ())), preferred_element_type=jnp.float32
            )

        @pl.when(y == 0)
        def _():
            total = jnp.zeros((ROUND_ROWS, rows), jnp.float32)
            for j in range(PIECES):
                lhs = (late[r, j].astype(jnp.float32) * factor[j]).astype(jnp.bfloat16)
                total = total + product(lhs, oth[j])
            slab[r] = total + extra[r]

        @pl.when(y == 1)
        def _():
            total = jnp.zeros((ROUND_ROWS, rows), jnp.float32)
            for j in range(PIECES):
                total = total + product(late[r, j], ready[j])
            slab[r] = total + extra[r]

    late_owners = owners(3)

    def deliver(r):
        for copy in shares(r):
            copy.wait_recv()
        total = slab[r, pl.ds(pl.multiple_of(c * share, share), share), :]
        for d in range(3):
            total = total + slab_in[r, d]
        late_piece[r] = total.astype(late_piece.dtype)
        for i, device in enumerate(late_owners):
            here = jnp.logical_and(device[0] == e, device[1] == c)
            spot = late_parts.at[r, c]

            @pl.when(here)
            def _():
                pltpu.make_async_copy(late_piece.at[r], spot, late_recv.at[r, c]).start()

            @pl.when(jnp.logical_not(here))
            def _():
                remote(late_piece.at[r], spot, lp_send.at[r, i], late_recv.at[r, c], device).start()

    def one_round(r, carry):
        remote(late.at[r], late.at[r], l_send.at[r], l_recv.at[r], behind).wait_recv()
        remote(extra.at[r], extra.at[r], t_send.at[r], t_recv.at[r], mate).wait_recv()
        multiply(r)
        for copy in shares(r):
            copy.start()

        @pl.when(r > 0)
        def _():
            deliver(r - 1)

        return carry

    lax.fori_loop(0, rounds, one_round, 0)
    deliver(rounds - 1)

    flag_copy.wait_recv()

    def part_wait(row, q):
        spot = parts.at[row, q]
        remote(spot, spot, p_send.at[0, 0], parts_recv.at[row, q], mate).wait_recv()

    def quarter_at(q):
        start = (q % 2) * half_rows + (q // 2) * quarter_rows
        return slice(start, start + quarter_rows)

    @pl.when(offset == 1)
    def _():
        for q in range(4):
            part_wait(0, q)
            part_wait(1, q)
            both = parts[0, q].astype(jnp.float32) + parts[1, q].astype(jnp.float32)
            turned[quarter_at(q), :] = both

    @pl.when(offset == 2)
    def _():
        for r in range(rounds):
            for q in range(4):
                spot = late_parts.at[r, q]
                remote(spot, spot, lp_send.at[0, 0], late_recv.at[r, q], mate).wait_recv()
                start = r * ROUND_ROWS + q * share
                turned[start : start + share, :] = late_parts[r, q].astype(jnp.float32)

    turn = (1 - x + (offset - 1) * (1 - odd)) % 2
    listed = flag_own[0:1, 0:1] * x.astype(jnp.float32) + flag_in[0:1, 0:1] * (1 - x).astype(jnp.float32)

    @pl.when(turn == 1)
    def _():
        out_ref[...] = turned[...].T * listed

    @pl.when(turn == 0)
    def _():
        out_ref[...] = turned[...] * listed

    for j in range(PIECES):
        y_copies[j].wait_send()
        e_copies[j].wait_send()
    flag_copy.wait_send()
    finish_early()
    for r in range(rounds):
        l_copies[r].wait_send()
        extra_copies[r].wait_send()
        for copy in shares(r):
            copy.wait_send()
        for i, device in enumerate(late_owners):
            here = jnp.logical_and(device[0] == e, device[1] == c)

            @pl.when(jnp.logical_not(here))
            def _():
                remote(
                    late_piece.at[r], late_parts.at[r, c], lp_send.at[r, i], late_recv.at[r, c], device
                ).wait_send()


def fused(grads, second_moment, step_size, partners, counts):
    rows, width = grads.shape[1:]
    reach = partners.shape[1]
    blocks = lax.axis_size("ex")
    piece_width = width // 2 // PIECES
    dma = pltpu.SemaphoreType.DMA
    vmem = pl.BlockSpec(memory_space=pltpu.VMEM)
    smem = pl.BlockSpec(memory_space=pltpu.SMEM)
    rounds, share = rows // ROUND_ROWS, ROUND_ROWS // 4
    gradients = pltpu.VMEM((PIECES, rows, piece_width), jnp.bfloat16)
    return pl.pallas_call(
        functools.partial(kernel, blocks, reach),
        out_shape=jax.ShapeDtypeStruct((rows, rows), jnp.float32),
        in_specs=[pl.BlockSpec(memory_space=pl.ANY), vmem, smem, smem, smem],
        out_specs=vmem,
        scratch_shapes=[
            gradients, gradients, gradients,
            pltpu.VMEM((rounds, PIECES, ROUND_ROWS, piece_width), jnp.bfloat16),
            pltpu.VMEM((PIECES, 1, piece_width), jnp.float32),
            pltpu.VMEM((3, rows, rows), jnp.float32),
            pltpu.VMEM((2, rows // 2, rows), jnp.float32),
            pltpu.VMEM((2, rows // 4, rows), jnp.float32),
            pltpu.VMEM((2, rows // 4, rows), jnp.bfloat16),
            pltpu.VMEM((2, rows // 2, rows), jnp.float32),
            pltpu.VMEM((2, rows // 4, rows), jnp.float32),
            pltpu.VMEM((2, 4, rows // 4, rows), jnp.bfloat16),
            pltpu.VMEM((8, 128), jnp.float32),
            pltpu.VMEM((8, 128), jnp.float32),
            pltpu.VMEM((rows, rows), jnp.float32),
            gradients,
            pltpu.VMEM((rounds, ROUND_ROWS, rows), jnp.float32),
            pltpu.VMEM((rounds, 3, share, rows), jnp.float32),
            pltpu.VMEM((rounds, share, rows), jnp.bfloat16),
            pltpu.VMEM((rounds, 4, share, rows), jnp.bfloat16),
            pltpu.VMEM((rounds, ROUND_ROWS, rows), jnp.float32),
            dma((PIECES,)), dma((PIECES,)), dma((PIECES,)), dma((PIECES,)), dma((PIECES,)),
            dma((rounds,)), dma((rounds,)),
            dma, dma, dma, dma, dma((2, 2)), dma((2, 4)),
            dma, dma,
            dma((rounds, 3)), dma((rounds, 3)), dma((rounds, 2)), dma((rounds, 4)),
            dma((rounds,)), dma((rounds,)),
        ],
        compiler_params=pltpu.CompilerParams(collective_id=0, has_side_effects=True),
    )(grads[0], second_moment, step_size, partners, counts)


def local(grads, second_moment, step_size, partners, counts):
    rows, width = grads.shape[1:]
    blocks, ckpts = lax.axis_size("ex"), lax.axis_size("ckpt")
    fits = partners.shape[1] == 2 and ckpts == 4 and blocks % 2 == 0 and blocks >= 6
    fits = fits and rows % 64 == 0 and width % (256 * PIECES) == 0
    body = fused if fits else general
    return body(grads, second_moment, step_size, partners, counts)


def solution(mesh):
    in_specs = (P("ckpt", "ex", None), P("ckpt", None), P("ckpt"), P("ex", None), P("ex"))
    out_specs = P("ex", "ckpt")
    return jax.shard_map(local, mesh=mesh, in_specs=in_specs, out_specs=out_specs, check_vma=False)
```

```python
import functools

import jax
import jax.numpy as jnp
from jax import lax
from jax.experimental import pallas as pl
from jax.experimental.pallas import tpu as pltpu
from jax.sharding import PartitionSpec as P

EPSILON = 1e-08
MESH = pl.DeviceIdType.MESH
PIECES = 4
ROUND_ROWS = 64


def passed_along(value, axis, by):
    length = lax.axis_size(axis)
    return lax.ppermute(value, axis, [(i, (i + by) % length) for i in range(length)])


def general(grads, second_moment, step_size, partners, counts):
    width = grads.shape[2]
    block_rows = grads.shape[1]
    reach = partners.shape[1]
    blocks = lax.axis_size("ex")
    position = lax.axis_index("ex")
    factor = step_size[:, None] / (jnp.sqrt(second_moment) + EPSILON) * width ** (-0.5)
    scaled = (grads.astype(jnp.float32) * factor[:, None, :]).astype(jnp.bfloat16)
    offsets = jnp.mod(partners[0] - position, blocks)
    alive_slot = jnp.arange(reach, dtype=jnp.int32) < counts[0]
    wanted = jnp.arange(1, reach + 1, dtype=jnp.int32)
    matched = jnp.logical_and(offsets[:, None] == wanted[None, :], alive_slot[:, None])
    listed = jnp.sum(matched.astype(jnp.float32), axis=0)
    forward_list = []
    for offset in range(1, reach + 1):
        visitor = passed_along(grads, "ex", -offset)
        forward_list.append(
            lax.dot_general(
                scaled, visitor, (((0, 2), (0, 2)), ((), ())), preferred_element_type=jnp.float32
            )
            * listed[offset - 1]
        )
    stacked = jnp.stack(forward_list, axis=1)
    returned = []
    for offset in range(reach, 0, -1):
        arrived = passed_along(stacked[:, offset - 1, :], "ex", offset)
        returned.append(arrived.T)
    panel = jnp.concatenate([jnp.stack(returned, axis=1), stacked], axis=1)
    panel = panel.reshape(block_rows, 2 * reach * block_rows)
    return lax.psum_scatter(panel, "ckpt", scatter_dimension=1, tiled=True)


def kernel(
    blocks, reach, g_ref, moment_ref, step_ref, partners_ref, counts_ref, out_ref,
    own, oth, early, late, factor, acc, half, quarter, piece, half_in, quarter_in, parts,
    flag_own, flag_in, turned, ready, slab, slab_in, late_piece, late_parts, extra,
    own_sem, y_send, y_recv, e_send, e_recv, l_send, l_recv,
    h_send, h_recv, q_send, q_recv, p_send, parts_recv, f_send, f_recv,
    x_send, x_recv, lp_send, late_recv, t_send, t_recv,
):
    rows, width = g_ref.shape
    layers = blocks // 2
    span = width // 2
    piece_width = span // PIECES
    half_rows, quarter_rows = rows // 2, rows // 4
    rounds, share = rows // ROUND_ROWS, ROUND_ROWS // 4
    e = lax.axis_index("ex")
    c = lax.axis_index("ckpt")
    z, y = e // 2, e % 2
    core, x = c % 2, c // 2

    mate = (2 * z + 1 - y, c)
    ahead = ((e + 2 * (2 * y - 1) + blocks) % blocks, c)
    behind = ((e - 2 * (2 * y - 1) + blocks) % blocks, c)
    core_mate = (e, c + 1 - 2 * core)
    x_mate = (e, (c + 2) % 4)
    cross_mate = (e, (c + 3 - 2 * core) % 4)
    offset = 2 - ((c + 1) // 2) % 2
    flag_to = ((e + offset) % blocks, c)
    flag_from = ((e - offset + blocks) % blocks, c)

    def owners(slot):
        a, o = [(2 * z, 1), (2 * z + 1 - 2 * y, 1), (2 * z - y, 2), (2 * z - 1 + y, 2)][slot]
        a = (a + blocks) % blocks
        return (a, reach - 1 + o), ((a + o) % blocks, reach - o)

    tile_row = (e - (1 - x) * offset + blocks) % blocks
    odd = tile_row % 2
    sources = []
    for row in range(2):
        layer = (tile_row // 2 + odd * ((offset - 1) + (2 - offset) * row)) % layers
        sources += [(2 * layer + row, q) for q in range(4)]

    barrier = pltpu.get_barrier_semaphore()

    for device in [mate, ahead, behind, core_mate, x_mate, cross_mate, flag_from] + sources:
        pl.semaphore_signal(barrier, inc=1, device_id=device, device_id_type=MESH)

    mine = pl.multiple_of(y * span, 128)
    theirs = pl.multiple_of((1 - y) * span, 128)
    own_copies = [
        pltpu.make_async_copy(
            g_ref.at[:, pl.ds(mine + j * piece_width, piece_width)], own.at[j], own_sem.at[j]
        )
        for j in range(PIECES)
    ]
    for copy in own_copies:
        copy.start()

    total = jnp.float32(0)
    for s in range(reach):
        apart = (partners_ref[0, s] - e + blocks) % blocks
        live = jnp.logical_and(apart == offset, s < counts_ref[0])
        total = total + jnp.where(live, jnp.float32(1), jnp.float32(0))
    flag_own[...] = jnp.full(flag_own.shape, total, jnp.float32)
    scale = step_ref[0] / (jnp.sqrt(moment_ref[:, pl.ds(mine, span)]) + EPSILON) * width ** (-0.5)
    for j in range(PIECES):
        factor[j] = scale[:, j * piece_width : (j + 1) * piece_width]

    pl.semaphore_wait(barrier, 15)

    def remote(src, dst, send, recv, device):
        return pltpu.make_async_remote_copy(
            src_ref=src, dst_ref=dst, send_sem=send, recv_sem=recv, device_id=device, device_id_type=MESH
        )

    flag_copy = remote(flag_own, flag_in, f_send, f_recv, flag_to)
    y_copies, e_copies, l_copies = [], [], []
    for j in range(PIECES):
        y_copies.append(
            remote(
                g_ref.at[:, pl.ds(theirs + j * piece_width, piece_width)],
                oth.at[j], y_send.at[j], y_recv.at[j], mate,
            )
        )
        e_copies.append(
            remote(
                g_ref.at[:, pl.ds(mine + j * piece_width, piece_width)],
                early.at[j], e_send.at[j], e_recv.at[j], ahead,
            )
        )
    for r in range(rounds):
        part = oth.at[:, pl.ds(r * ROUND_ROWS, ROUND_ROWS), :]
        l_copies.append(remote(part, late.at[r], l_send.at[r], l_recv.at[r], behind))
    for j in range(PIECES):
        y_copies[j].start()
        e_copies[j].start()
    flag_copy.start()

    def scaled(ref, j):
        return (ref[j].astype(jnp.float32) * factor[j]).astype(jnp.bfloat16)

    def add(slot, lhs, rhs, first):
        product = lax.dot_general(
            lhs, rhs, (((1,), (1,)), ((), ())), preferred_element_type=jnp.float32
        )
        if first:
            acc[slot] = product
        else:
            acc[slot] += product

    def tiles(todo, j, first):
        @pl.when(y == 0)
        def _():
            for slot, left, right in todo:
                if slot == 2:
                    add(slot, right[j], scaled(left, j), first)
                else:
                    add(slot, scaled(left, j), right[j], first)

        @pl.when(y == 1)
        def _():
            for slot, left, right in todo:
                add(slot, scaled(right, j), left[j], first)

    def over_pieces(todo, arrive):
        arrive(0)
        tiles(todo, 0, True)

        def body(j, carry):
            arrive(j)
            tiles(todo, j, False)
            return carry

        lax.fori_loop(1, PIECES, body, 0)

    for copy in own_copies:
        copy.wait()

    def y_arrive(j):
        remote(oth.at[j], oth.at[j], y_send.at[j], y_recv.at[j], mate).wait_recv()

    def wait_piece(j, carry):
        y_arrive(j)
        return carry

    lax.fori_loop(0, PIECES, wait_piece, 0)
    for copy in l_copies:
        copy.start()
    over_pieces([(0, own, oth)], lambda j: None)

    def e_arrive(j):
        remote(early.at[j], early.at[j], e_send.at[j], e_recv.at[j], ahead).wait_recv()

    over_pieces([(2, own, early), (1, oth, early)], e_arrive)
    extra_copies = []
    for r in range(rounds):
        part = pl.ds(r * ROUND_ROWS, ROUND_ROWS)
        extra_copies.append(remote(acc.at[2, part, :], extra.at[r], t_send.at[r], t_recv.at[r], mate))
    for copy in extra_copies:
        copy.start()

    def reduce_and_deliver(slots):
        low, high = slots[0], len(slots)
        group = pl.ds(low, high)
        keep = pl.multiple_of(core * half_rows, 16)
        give = pl.multiple_of((1 - core) * half_rows, 16)
        for t in slots:
            half[t] = acc[t, pl.ds(give, half_rows), :]
        first = remote(half.at[group], half_in.at[group], h_send, h_recv, core_mate)
        first.start()
        first.wait_recv()
        keep_x = pl.multiple_of(x * quarter_rows, 16)
        give_x = pl.multiple_of((1 - x) * quarter_rows, 16)
        for t in slots:
            quarter[t] = acc[t, pl.ds(keep + give_x, quarter_rows), :] + half_in[t, pl.ds(give_x, quarter_rows), :]
        second = remote(
            quarter.at[group], quarter_in.at[group], q_send, q_recv, x_mate
        )
        second.start()
        second.wait_recv()
        for t in slots:
            kept = acc[t, pl.ds(keep + keep_x, quarter_rows), :] + half_in[t, pl.ds(keep_x, quarter_rows), :]
            piece[t] = (kept + quarter_in[t]).astype(piece.dtype)
        for t in slots:
            for i, device in enumerate(owners(t)):
                here = jnp.logical_and(device[0] == e, device[1] == c)
                spot = parts.at[y, c]

                @pl.when(here)
                def _():
                    pltpu.make_async_copy(piece.at[t], spot, parts_recv.at[y, c]).start()

                @pl.when(jnp.logical_not(here))
                def _():
                    remote(piece.at[t], spot, p_send.at[t, i], parts_recv.at[y, c], device).start()

        def finish():
            first.wait_send()
            second.wait_send()
            for t in slots:
                for i, device in enumerate(owners(t)):
                    here = jnp.logical_and(device[0] == e, device[1] == c)

                    @pl.when(jnp.logical_not(here))
                    def _():
                        remote(
                            piece.at[t], parts.at[y, c], p_send.at[t, i], parts_recv.at[y, c], device
                        ).wait_send()

        return finish

    finish_early = reduce_and_deliver((0, 1))

    @pl.when(y == 1)
    def _():
        def scale_piece(j, carry):
            ready[j] = (oth[j].astype(jnp.float32) * factor[j]).astype(jnp.bfloat16)
            return carry

        lax.fori_loop(0, PIECES, scale_piece, 0)

    def shares(r):
        out = []
        for d in range(1, 4):
            peer = (c + d) % 4
            given = slab.at[r, pl.ds(pl.multiple_of(peer * share, share), share), :]
            out.append(
                remote(given, slab_in.at[r, d - 1], x_send.at[r, d - 1], x_recv.at[r, d - 1], (e, peer))
            )
        return out

    def multiply(r):
        def product(lhs, rhs):
            return lax.dot_general(
                lhs, rhs, (((1,), (1,)), ((), ())), preferred_element_type=jnp.float32
            )

        @pl.when(y == 0)
        def _():
            total = jnp.zeros((ROUND_ROWS, rows), jnp.float32)
            for j in range(PIECES):
                lhs = (late[r, j].astype(jnp.float32) * factor[j]).astype(jnp.bfloat16)
                total = total + product(lhs, oth[j])
            slab[r] = total + extra[r]

        @pl.when(y == 1)
        def _():
            total = jnp.zeros((ROUND_ROWS, rows), jnp.float32)
            for j in range(PIECES):
                total = total + product(late[r, j], ready[j])
            slab[r] = total + extra[r]

    late_owners = owners(3)

    def deliver(r):
        for copy in shares(r):
            copy.wait_recv()
        total = slab[r, pl.ds(pl.multiple_of(c * share, share), share), :]
        for d in range(3):
            total = total + slab_in[r, d]
        late_piece[r] = total.astype(late_piece.dtype)
        for i, device in enumerate(late_owners):
            here = jnp.logical_and(device[0] == e, device[1] == c)
            spot = late_parts.at[r, c]

            @pl.when(here)
            def _():
                pltpu.make_async_copy(late_piece.at[r], spot, late_recv.at[r, c]).start()

            @pl.when(jnp.logical_not(here))
            def _():
                remote(late_piece.at[r], spot, lp_send.at[r, i], late_recv.at[r, c], device).start()

    def one_round(r, carry):
        remote(late.at[r], late.at[r], l_send.at[r], l_recv.at[r], behind).wait_recv()
        remote(extra.at[r], extra.at[r], t_send.at[r], t_recv.at[r], mate).wait_recv()
        multiply(r)
        for copy in shares(r):
            copy.start()

        @pl.when(r > 0)
        def _():
            deliver(r - 1)

        return carry

    lax.fori_loop(0, rounds, one_round, 0)
    deliver(rounds - 1)

    flag_copy.wait_recv()

    def part_wait(row, q):
        spot = parts.at[row, q]
        remote(spot, spot, p_send.at[0, 0], parts_recv.at[row, q], mate).wait_recv()

    def quarter_at(q):
        start = (q % 2) * half_rows + (q // 2) * quarter_rows
        return slice(start, start + quarter_rows)

    @pl.when(offset == 1)
    def _():
        for q in range(4):
            part_wait(0, q)
            part_wait(1, q)
            both = parts[0, q].astype(jnp.float32) + parts[1, q].astype(jnp.float32)
            turned[quarter_at(q), :] = both

    @pl.when(offset == 2)
    def _():
        for r in range(rounds):
            for q in range(4):
                spot = late_parts.at[r, q]
                remote(spot, spot, lp_send.at[0, 0], late_recv.at[r, q], mate).wait_recv()
                start = r * ROUND_ROWS + q * share
                turned[start : start + share, :] = late_parts[r, q].astype(jnp.float32)

    turn = (1 - x + (offset - 1) * (1 - odd)) % 2
    listed = flag_own[0:1, 0:1] * x.astype(jnp.float32) + flag_in[0:1, 0:1] * (1 - x).astype(jnp.float32)

    @pl.when(turn == 1)
    def _():
        out_ref[...] = turned[...].T * listed

    @pl.when(turn == 0)
    def _():
        out_ref[...] = turned[...] * listed

    for j in range(PIECES):
        y_copies[j].wait_send()
        e_copies[j].wait_send()
    flag_copy.wait_send()
    finish_early()
    for r in range(rounds):
        l_copies[r].wait_send()
        extra_copies[r].wait_send()
        for copy in shares(r):
            copy.wait_send()
        for i, device in enumerate(late_owners):
            here = jnp.logical_and(device[0] == e, device[1] == c)

            @pl.when(jnp.logical_not(here))
            def _():
                remote(
                    late_piece.at[r], late_parts.at[r, c], lp_send.at[r, i], late_recv.at[r, c], device
                ).wait_send()


def fused(grads, second_moment, step_size, partners, counts):
    rows, width = grads.shape[1:]
    reach = partners.shape[1]
    blocks = lax.axis_size("ex")
    piece_width = width // 2 // PIECES
    dma = pltpu.SemaphoreType.DMA
    vmem = pl.BlockSpec(memory_space=pltpu.VMEM)
    smem = pl.BlockSpec(memory_space=pltpu.SMEM)
    rounds, share = rows // ROUND_ROWS, ROUND_ROWS // 4
    gradients = pltpu.VMEM((PIECES, rows, piece_width), jnp.bfloat16)
    return pl.pallas_call(
        functools.partial(kernel, blocks, reach),
        out_shape=jax.ShapeDtypeStruct((rows, rows), jnp.float32),
        in_specs=[pl.BlockSpec(memory_space=pl.ANY), vmem, smem, smem, smem],
        out_specs=vmem,
        scratch_shapes=[
            gradients, gradients, gradients,
            pltpu.VMEM((rounds, PIECES, ROUND_ROWS, piece_width), jnp.bfloat16),
            pltpu.VMEM((PIECES, 1, piece_width), jnp.float32),
            pltpu.VMEM((3, rows, rows), jnp.float32),
            pltpu.VMEM((2, rows // 2, rows), jnp.float32),
            pltpu.VMEM((2, rows // 4, rows), jnp.float32),
            pltpu.VMEM((2, rows // 4, rows), jnp.bfloat16),
            pltpu.VMEM((2, rows // 2, rows), jnp.float32),
            pltpu.VMEM((2, rows // 4, rows), jnp.float32),
            pltpu.VMEM((2, 4, rows // 4, rows), jnp.bfloat16),
            pltpu.VMEM((8, 128), jnp.float32),
            pltpu.VMEM((8, 128), jnp.float32),
            pltpu.VMEM((rows, rows), jnp.float32),
            gradients,
            pltpu.VMEM((rounds, ROUND_ROWS, rows), jnp.float32),
            pltpu.VMEM((rounds, 3, share, rows), jnp.float32),
            pltpu.VMEM((rounds, share, rows), jnp.bfloat16),
            pltpu.VMEM((rounds, 4, share, rows), jnp.bfloat16),
            pltpu.VMEM((rounds, ROUND_ROWS, rows), jnp.float32),
            dma((PIECES,)), dma((PIECES,)), dma((PIECES,)), dma((PIECES,)), dma((PIECES,)),
            dma((rounds,)), dma((rounds,)),
            dma, dma, dma, dma, dma((2, 2)), dma((2, 4)),
            dma, dma,
            dma((rounds, 3)), dma((rounds, 3)), dma((rounds, 2)), dma((rounds, 4)),
            dma((rounds,)), dma((rounds,)),
        ],
        compiler_params=pltpu.CompilerParams(collective_id=0, has_side_effects=True),
    )(grads[0], second_moment, step_size, partners, counts)


def local(grads, second_moment, step_size, partners, counts):
    rows, width = grads.shape[1:]
    blocks, ckpts = lax.axis_size("ex"), lax.axis_size("ckpt")
    fits = partners.shape[1] == 2 and ckpts == 4 and blocks % 2 == 0 and blocks >= 6
    fits = fits and rows % 64 == 0 and width % (256 * PIECES) == 0
    body = fused if fits else general
    return body(grads, second_moment, step_size, partners, counts)


def solution(mesh):
    in_specs = (P("ckpt", "ex", None), P("ckpt", None), P("ckpt"), P("ex", None), P("ex"))
    out_specs = P("ex", "ckpt")
    return jax.shard_map(local, mesh=mesh, in_specs=in_specs, out_specs=out_specs, check_vma=False)
```
